32 devices in a mesh: node: 4 (over y, x), feat: 4 (over z), tm: 2 (over core).
Axes of the slice: x: 2, y: 2, z: 4, core: 2. Of those that a mesh axis runs over, the one named last changes fastest.
Arguments:
- tensor: float32 [2, 16384, 4096], P('tm', 'node', 'feat'), may hold values from -6 to 6
- basis: float32 [16384, 128], P('node'), may hold values from -0.046875 to 0.046875
Outputs:
- gram: float32 [4096, 4096], P('feat', ('node', 'tm'))
The draws below stay inside these ranges and needn't reach their ends.
All inputs are finite; a program needn't handle non-finite values.
Results may differ from the reference program's by a relative error of at most 0.000073.
Values sent between devices are 32-bit elements; how exact they have to be, the bound alone decides.
No kernel may reach another device: no remote copies, remote signals or barrier semaphores. Data moves between devices by JAX's collectives and lax.ppermute only.
A program may use at most 128 MiB of HBM per device.

```python
import jax
import jax.numpy as jnp
from jax import lax

FEAT = 4096
R = 128
NODES = 16384
TIME = 2


def shard_levels(own_key, dims, pieces, least, top_value):
    gain = 1.0
    for position, parts in pieces:
        steps = jax.random.uniform(jax.random.fold_in(jax.random.fold_in(own_key, 6), position), (parts,), jnp.float32, least / len(pieces), top_value / len(pieces))
        gain = gain * jnp.repeat(jnp.exp(steps), dims[position] // parts).reshape((-1,) + (1,) * (len(dims) - 1 - position))
    return gain


def gaussian(key, dims, scale, limit, pieces=(), dtype=jnp.bfloat16):
    level = shard_levels(key, dims, pieces, -0.22, 0.18) if pieces else 1.0
    result = jax.random.normal(key, dims, jnp.float32) * scale * level
    return jnp.minimum(jnp.maximum(result, -limit), limit).astype(dtype)


def setup_inputs(seed: int = 0) -> dict:
    key_of = jax.random.split(jax.random.key(seed), 3)
    return {
        "tensor": gaussian(key_of[0], (TIME, NODES, FEAT), 1.0, 6.0, ((0, 2), (1, 4), (2, 4)), jnp.float32),
        "basis": gaussian(key_of[1], (NODES, R), NODES ** -0.5, 0.046875, ((0, 4),), jnp.float32),
    }


def reference(tensor, basis):
    projected = jnp.einsum("nr,tnf->rft", basis, tensor, precision=lax.Precision.HIGHEST)
    gram = jnp.einsum("rft,rgt->fg", projected, projected, precision=lax.Precision.HIGHEST)
    return gram * (1.0 / (R * TIME))
```

```python
import jax
import jax.numpy as jnp
from jax import lax
from jax.sharding import PartitionSpec as P

TM_SWAP = [(0, 1), (1, 0)]


def body(tensor, basis):
    nodes = lax.axis_size("node")
    feats = lax.axis_size("feat")
    times = lax.axis_size("tm")
    rank = basis.shape[1]
    width = tensor.shape[2]
    groups = nodes // feats
    rows = rank // nodes
    cols = width // (groups * times)
    scale = 1.0 / (rank * times)

    partial = lax.dot_general(
        basis,
        tensor[0],
        (((0,), (0,)), ((), ())),
        precision=lax.Precision.HIGH,
        preferred_element_type=jnp.float32,
    )

    pieces = partial.reshape(nodes, rows, groups, times, cols).transpose(0, 3, 1, 2, 4)
    pieces = pieces.reshape(nodes * times, rows, groups * cols)
    pieces = lax.all_to_all(pieces, ("node", "tm"), 0, 0, tiled=True)
    share = jnp.sum(pieces.reshape(nodes, times * rows, groups * cols), axis=0)

    blocks = lax.all_gather(share, "feat", axis=0, tiled=False)
    right = blocks.reshape(feats, times * rows, groups, cols).transpose(0, 2, 1, 3)
    right = right.reshape(nodes, times * rows, cols)
    left = jnp.broadcast_to(share[None], (nodes, times * rows, groups * cols))
    both = lax.all_to_all(jnp.concatenate([left, right], axis=2), "node", 0, 0, tiled=True)
    depth = nodes * times * rows
    left = both[:, :, : groups * cols].reshape(depth, groups * cols)
    right = both[:, :, groups * cols :].reshape(depth, cols)

    other = lax.ppermute(left, "tm", TM_SWAP)
    core = lax.axis_index("tm")
    even = jnp.where(core == 0, left, other).reshape(depth, groups, 1, cols)
    odd = jnp.where(core == 0, other, left).reshape(depth, groups, 1, cols)
    full = jnp.concatenate([even, odd], axis=2).reshape(depth, width)
    gram = lax.dot_general(
        full,
        right,
        (((0,), (0,)), ((), ())),
        precision=lax.Precision.HIGH,
        preferred_element_type=jnp.float32,
    )
    return gram * scale


def solution(mesh):
    in_specs = (P("tm", "node", "feat"), P("node", None))
    out_specs = P("feat", ("node", "tm"))
    return jax.shard_map(body, mesh=mesh, in_specs=in_specs, out_specs=out_specs, check_vma=False)
```

```python
import functools

import jax
import jax.numpy as jnp
from jax import lax
from jax.experimental import pallas as pl
from jax.experimental.pallas import tpu as pltpu
from jax.sharding import PartitionSpec as P

VMEM_LIMIT = 48 * 1024 * 1024


def split(x):
    high = x.astype(jnp.bfloat16)
    return high, (x - high.astype(jnp.float32)).astype(jnp.bfloat16)


def project_kernel(cols, chunk, basis_hbm, tensor_hbm, out, basis, tensor, factor, total, basis_sem, tensor_sem):
    depth, width = tensor.shape
    rank = basis.shape[1]
    nodes, cores, rows, _ = out.shape
    count = depth // chunk

    def basis_copy(k):
        part = pl.ds(k * chunk, chunk)
        return pltpu.make_async_copy(basis_hbm.at[part], basis.at[part], basis_sem.at[k])

    def tensor_copy(k):
        part = pl.ds(k * chunk, chunk)
        return pltpu.make_async_copy(tensor_hbm.at[0, part], tensor.at[part], tensor_sem.at[k])

    for k in range(count):
        basis_copy(k).start()
        tensor_copy(k).start()
    for k in range(count):
        part = slice(k * chunk, (k + 1) * chunk)
        basis_copy(k).wait()
        high, low = split(basis[part].T)
        factor[:rank, part] = high
        factor[rank:, part] = low
        tensor_copy(k).wait()
        high, low = split(tensor[part])
        first = jnp.dot(factor[:, part], high, preferred_element_type=jnp.float32)
        second = jnp.dot(factor[:rank, part], low, preferred_element_type=jnp.float32)
        term = first[:rank] + first[rank:] + second
        if k == 0:
            total[...] = term
        else:
            total[...] += term
    for g in range(width // (cores * cols)):
        for c in range(cores):
            start = (g * cores + c) * cols
            value = total[:, start : start + cols]
            out[:, c, :, g * cols : (g + 1) * cols] = value.reshape(nodes, rows, cols)


def project(tensor, basis, nodes, cores, groups, cols):
    _, depth, width = tensor.shape
    rank = basis.shape[1]
    chunk = depth // 8
    return pl.pallas_call(
        functools.partial(project_kernel, cols, chunk),
        in_specs=[pl.BlockSpec(memory_space=pl.ANY)] * 2,
        out_specs=pl.BlockSpec(memory_space=pltpu.VMEM),
        out_shape=jax.ShapeDtypeStruct((nodes, cores, rank // nodes, groups * cols), jnp.float32),
        scratch_shapes=[
            pltpu.VMEM((depth, rank), jnp.float32),
            pltpu.VMEM((depth, width), jnp.float32),
            pltpu.VMEM((2 * rank, depth), jnp.bfloat16),
            pltpu.VMEM((rank, width), jnp.float32),
            pltpu.SemaphoreType.DMA((8,)),
            pltpu.SemaphoreType.DMA((8,)),
        ],
        compiler_params=pltpu.CompilerParams(vmem_limit_bytes=VMEM_LIMIT),
        cost_estimate=pl.CostEstimate(
            flops=6 * rank * depth * width, bytes_accessed=4 * depth * (width + rank), transcendentals=0
        ),
        name="project",
    )(basis, tensor)


def gram_kernel(nodes, groups, cols, scale, place, *refs):
    own, other, come = refs[:nodes], refs[nodes : 2 * nodes], refs[2 * nodes : 3 * nodes]
    out, high_scr, low_scr = refs[3 * nodes :]
    rows = own[0].shape[0]
    step = pl.program_id(0)
    local = place[2] == 1

    @pl.when((step == 0) & local)
    def _():
        part = pl.ds(pl.multiple_of(place[1] * cols, cols), cols)
        for d in range(nodes):
            high, low = split(own[d][:, part])
            high_scr[d * rows : (d + 1) * rows] = high
            low_scr[d * rows : (d + 1) * rows] = low

    @pl.when((step == 0) & jnp.logical_not(local))
    def _():
        for p in range(nodes):
            high, low = split(come[p][...])
            part = pl.ds(pl.multiple_of(place[3 + p] * rows, rows), rows)
            high_scr[part] = high
            low_scr[part] = low

    def product(left, g):
        value = jnp.concatenate([ref[:, g * cols : (g + 1) * cols] for ref in left], axis=0)
        high, low = split(value.T)
        term = jnp.dot(high, high_scr[...], preferred_element_type=jnp.float32)
        term += jnp.dot(low, high_scr[...], preferred_element_type=jnp.float32)
        term += jnp.dot(high, low_scr[...], preferred_element_type=jnp.float32)
        out[...] = term * scale

    for g in range(groups):
        for side, left in enumerate((own, other)):
            pl.when(step == g * 2 + side)(functools.partial(product, left, g))


def gram_block(place, own, other, come, groups, cols, scale):
    nodes = len(own)
    rows, width = own[0].shape
    depth = nodes * rows
    whole = lambda shape: pl.BlockSpec(shape, lambda s, place: (0, 0))
    core_first = lambda s, place: ((s // 2) * 2 + (place[0] + s % 2) % 2, 0)
    return pl.pallas_call(
        functools.partial(gram_kernel, nodes, groups, cols, scale),
        grid_spec=pltpu.PrefetchScalarGridSpec(
            num_scalar_prefetch=1,
            grid=(2 * groups,),
            in_specs=[whole((rows, width))] * (2 * nodes) + [whole((rows, cols))] * nodes,
            out_specs=pl.BlockSpec((cols, cols), core_first),
            scratch_shapes=[pltpu.VMEM((depth, cols), jnp.bfloat16)] * 2,
        ),
        out_shape=jax.ShapeDtypeStruct((2 * width, cols), jnp.float32),
        compiler_params=pltpu.CompilerParams(vmem_limit_bytes=VMEM_LIMIT),
        cost_estimate=pl.CostEstimate(
            flops=12 * depth * width * cols, bytes_accessed=8 * width * cols, transcendentals=0
        ),
        name="gram",
    )(place, *own, *other, *come)


def body(tensor, basis):
    nodes, feats, cores = lax.axis_size("node"), lax.axis_size("feat"), lax.axis_size("tm")
    rank = basis.shape[1]
    width = tensor.shape[2]
    groups = nodes // feats
    rows = rank // nodes
    cols = width // (groups * cores)
    scale = 1.0 / (rank * cores)
    node, feat, core = lax.axis_index("node"), lax.axis_index("feat"), lax.axis_index("tm")

    pieces = project(tensor, basis, nodes, cores, groups, cols)
    pieces = pieces.reshape(nodes * cores, rows, groups * cols)
    pieces = lax.all_to_all(pieces, ("node", "tm"), 0, 0, tiled=True)
    share = jnp.sum(pieces.reshape(nodes, cores * rows, groups * cols), axis=0)

    own = [share]
    for d in range(1, nodes):
        own.append(lax.ppermute(share, "node", [(n, n ^ d) for n in range(nodes)]))

    targets = (feats - 1) * groups
    come = []
    for p in range(nodes):
        pairs = []
        for z in range(feats):
            for idx in range(targets):
                source = (z * groups) ^ ((p + idx) % nodes)
                d, g = idx // groups + 1, idx % groups
                pairs.append((source * feats + z, (z * groups + g) * feats + (z ^ d)))
        if groups == 1:
            part = share
        else:
            g = ((node ^ (feat * groups)) - p) % nodes % groups
            part = lax.dynamic_slice_in_dim(share, g * cols, cols, 1)
        come.append(lax.ppermute(part, ("node", "feat"), pairs))

    other = [lax.ppermute(x, "tm", [(0, 1), (1, 0)]) for x in own]
    block, g = node // groups, node % groups
    idx = ((feat ^ block) - 1) * groups + g
    slots = [(((p + idx) % nodes) ^ (block * groups)) ^ node for p in range(nodes)]
    place = jnp.stack([core, g, (block == feat).astype(jnp.int32), *slots]).astype(jnp.int32)
    return gram_block(place, own, other, come, groups, cols, scale)


def solution(mesh):
    in_specs = (P("tm", "node", "feat"), P("node", None))
    out_specs = P("feat", ("node", "tm"))
    return jax.shard_map(body, mesh=mesh, in_specs=in_specs, out_specs=out_specs, check_vma=False)
```

```python
import functools

import jax
import jax.numpy as jnp
from jax import lax
from jax.experimental import pallas as pl
from jax.experimental.pallas import tpu as pltpu
from jax.sharding import PartitionSpec as P

VMEM_LIMIT = 56 * 1024 * 1024


def split(x):
    high = x.astype(jnp.bfloat16)
    return high, (x - high.astype(jnp.float32)).astype(jnp.bfloat16)


def project_kernel(chunk, basis_hbm, tensor_hbm, out, basis, tensor, factor, total, basis_sem, tensor_sem):
    depth, width = tensor.shape
    rank = basis.shape[1]
    nodes, rows, _ = out.shape
    count = depth // chunk

    def basis_copy(k):
        part = pl.ds(k * chunk, chunk)
        return pltpu.make_async_copy(basis_hbm.at[part], basis.at[part], basis_sem.at[k])

    def tensor_copy(k):
        part = pl.ds(k * chunk, chunk)
        return pltpu.make_async_copy(tensor_hbm.at[0, part], tensor.at[part], tensor_sem.at[k])

    for k in range(count):
        basis_copy(k).start()
        tensor_copy(k).start()
    for k in range(count):
        part = slice(k * chunk, (k + 1) * chunk)
        basis_copy(k).wait()
        high, low = split(basis[part].T)
        factor[:rank, part] = high
        factor[rank:, part] = low
        tensor_copy(k).wait()
        high, low = split(tensor[part])
        first = jnp.dot(factor[:, part], high, preferred_element_type=jnp.float32)
        second = jnp.dot(factor[:rank, part], low, preferred_element_type=jnp.float32)
        term = first[:rank] + first[rank:] + second
        if k == 0:
            total[...] = term
        else:
            total[...] += term
    out[...] = total[...].reshape(nodes, rows, width)


def project(tensor, basis, nodes):
    _, depth, width = tensor.shape
    rank = basis.shape[1]
    chunk = depth // 8
    return pl.pallas_call(
        functools.partial(project_kernel, chunk),
        in_specs=[pl.BlockSpec(memory_space=pl.ANY)] * 2,
        out_specs=pl.BlockSpec(memory_space=pltpu.VMEM),
        out_shape=jax.ShapeDtypeStruct((nodes, rank // nodes, width), jnp.float32),
        scratch_shapes=[
            pltpu.VMEM((depth, rank), jnp.float32),
            pltpu.VMEM((depth, width), jnp.float32),
            pltpu.VMEM((2 * rank, depth), jnp.bfloat16),
            pltpu.VMEM((rank, width), jnp.float32),
            pltpu.SemaphoreType.DMA((8,)),
            pltpu.SemaphoreType.DMA((8,)),
        ],
        compiler_params=pltpu.CompilerParams(vmem_limit_bytes=VMEM_LIMIT),
        cost_estimate=pl.CostEstimate(
            flops=6 * rank * depth * width, bytes_accessed=4 * depth * (width + rank), transcendentals=0
        ),
        name="project",
    )(basis, tensor)


def gram_kernel(nodes, groups, cols, scale, place, *refs):
    half = nodes // 2
    share, refs = refs[0], refs[1:]
    near, near_swap, refs = refs[: half - 1], refs[half - 1 : nodes - 2], refs[nodes - 2 :]
    far, far_swap, refs = refs[0], refs[1], refs[2:]
    come, come_swap, refs = refs[:half], refs[half:nodes], refs[nodes:]
    out, left, right_high, right_low = refs
    rows, width = share.shape
    step = pl.program_id(0)
    core = place[0]

    def slot(index):
        return pl.ds(pl.multiple_of(index * rows, rows), rows)

    def columns(index, size):
        return pl.ds(pl.multiple_of(index * size, size), size)

    @pl.when(step == 0)
    def _():
        left[:rows] = share[...]
        for k in range(half - 1):
            left[slot(2 * k + 1 + core)] = near[k][...]
            left[slot(2 * k + 2 - core)] = near_swap[k][...]
        left[(nodes - 1) * rows :, columns(core, width // 2)] = far[...]
        left[(nodes - 1) * rows :, columns(1 - core, width // 2)] = far_swap[...]

    @pl.when((step == 0) & (place[2] == 1))
    def _():
        high, low = split(left[:, columns(place[1] * 2 + core, cols)])
        right_high[...] = high
        right_low[...] = low

    @pl.when((step == 0) & (place[2] != 1))
    def _():
        for k in range(half):
            high, low = split(come[k][:, columns(core, cols)])
            right_high[slot(place[3 + k])] = high
            right_low[slot(place[3 + k])] = low
            high, low = split(come_swap[k][...])
            right_high[slot(place[3 + half + k])] = high
            right_low[slot(place[3 + half + k])] = low

    size = out.shape[0]
    high, low = split(left[:, columns(step, size)].T)
    term = jnp.dot(high, right_high[...], preferred_element_type=jnp.float32)
    term += jnp.dot(low, right_high[...], preferred_element_type=jnp.float32)
    term += jnp.dot(high, right_low[...], preferred_element_type=jnp.float32)
    out[...] = term * scale


def gram_block(place, share, near, near_swap, far, far_swap, come, come_swap, nodes, groups, cols, scale):
    rows, width = share.shape
    depth = nodes * rows
    size = width // 2
    arrays = (share, *near, *near_swap, far, far_swap, *come, *come_swap)
    return pl.pallas_call(
        functools.partial(gram_kernel, nodes, groups, cols, scale),
        grid_spec=pltpu.PrefetchScalarGridSpec(
            num_scalar_prefetch=1,
            grid=(width // size,),
            in_specs=[pl.BlockSpec(x.shape, lambda s, place: (0, 0)) for x in arrays],
            out_specs=pl.BlockSpec((size, cols), lambda s, place: (s, 0)),
            scratch_shapes=[
                pltpu.VMEM((depth, width), jnp.float32),
                pltpu.VMEM((depth, cols), jnp.bfloat16),
                pltpu.VMEM((depth, cols), jnp.bfloat16),
            ],
        ),
        out_shape=jax.ShapeDtypeStruct((width, cols), jnp.float32),
        compiler_params=pltpu.CompilerParams(vmem_limit_bytes=24 * 1024 * 1024),
        cost_estimate=pl.CostEstimate(
            flops=6 * depth * width * cols, bytes_accessed=4 * width * cols, transcendentals=0
        ),
        name="gram",
    )(place, *arrays)


def gray(n):
    return n ^ (n >> 1)


def body(tensor, basis):
    nodes, feats, cores = lax.axis_size("node"), lax.axis_size("feat"), lax.axis_size("tm")
    rank = basis.shape[1]
    width = tensor.shape[2]
    groups = nodes // feats
    rows = rank // nodes
    cols = width // (groups * cores)
    scale = 1.0 / (rank * cores)
    half = nodes // 2
    node, feat, core = lax.axis_index("node"), lax.axis_index("feat"), lax.axis_index("tm")
    everyone = ("node", "feat", "tm")

    def device(n, z, c):
        return (n * feats + z) * cores + c

    def swap(x):
        return lax.ppermute(x, "tm", [(0, 1), (1, 0)])

    pieces = lax.all_to_all(project(tensor, basis, nodes), "node", 0, 0, tiled=True)
    share = lax.all_gather(jnp.sum(pieces, axis=0), "tm", axis=0, tiled=True)

    targets = (feats - 1) * groups
    table = [0] * nodes
    for idx in range(targets):
        table[gray(idx)] = idx % groups
    come = []
    for k in range(half):
        pairs = []
        for c in range(cores):
            for z in range(feats):
                for idx in range(targets):
                    source = (z * groups) ^ (k + c * half) ^ gray(idx)
                    d, g = idx // groups + 1, idx % groups
                    pairs.append((device(source, z, c), device(z * groups + g, z ^ d, c)))
        if groups == 1:
            part = share
        else:
            g = jnp.asarray(table)[node ^ (feat * groups) ^ (k + core * half)]
            part = lax.dynamic_slice_in_dim(share, g * cores * cols, cores * cols, 1)
        come.append(lax.ppermute(part, everyone, pairs))

    near = []
    for k in range(half - 1):
        pairs = [
            (device(n, z, c), device(n ^ (2 * k + 1 + c), z, c))
            for c in range(cores)
            for n in range(nodes)
            for z in range(feats)
        ]
        near.append(lax.ppermute(share, everyone, pairs))
    part = lax.dynamic_slice_in_dim(share, core * (width // 2), width // 2, 1)
    far = lax.ppermute(part, "node", [(n, n ^ (nodes - 1)) for n in range(nodes)])

    near_swap = [swap(x) for x in near]
    far_swap = swap(far)
    come_swap = [swap(lax.dynamic_slice_in_dim(x, (1 - core) * cols, cols, 1)) for x in come]

    block, g = node // groups, node % groups
    idx = ((feat ^ block) - 1) * groups + g
    base = gray(idx) ^ (block * groups) ^ node
    slots = [(k + core * half) ^ base for k in range(half)] + [(k + (1 - core) * half) ^ base for k in range(half)]
    place = jnp.stack([core, g, (block == feat).astype(jnp.int32), *slots]).astype(jnp.int32)
    return gram_block(place, share, near, near_swap, far, far_swap, come, come_swap, nodes, groups, cols, scale)


def solution(mesh):
    in_specs = (P("tm", "node", "feat"), P("node", None))
    out_specs = P("feat", ("node", "tm"))
    return jax.shard_map(body, mesh=mesh, in_specs=in_specs, out_specs=out_specs, check_vma=False)
```

```python
import functools

import jax
import jax.numpy as jnp
from jax import lax
from jax.experimental import pallas as pl
from jax.experimental.pallas import tpu as pltpu
from jax.sharding import PartitionSpec as P

VMEM_LIMIT = 52 * 1024 * 1024


def split(x):
    high = x.astype(jnp.bfloat16)
    return high, (x - high.astype(jnp.float32)).astype(jnp.bfloat16)


def project_kernel(chunk, nodes, node, basis_hbm, tensor_hbm, *refs):
    outs = refs[:nodes]
    basis, tensor, factor, total, basis_sem, tensor_sem = refs[nodes:]
    depth, width = tensor.shape
    rank = basis.shape[1]
    rows = rank // nodes
    count = depth // chunk

    def basis_copy(k):
        part = pl.ds(k * chunk, chunk)
        return pltpu.make_async_copy(basis_hbm.at[part], basis.at[part], basis_sem.at[k])

    def tensor_copy(k):
        part = pl.ds(k * chunk, chunk)
        return pltpu.make_async_copy(tensor_hbm.at[0, part], tensor.at[part], tensor_sem.at[k])

    for k in range(count):
        basis_copy(k).start()
        tensor_copy(k).start()
    for k in range(count):
        part = slice(k * chunk, (k + 1) * chunk)
        basis_copy(k).wait()
        high, low = split(basis[part].T)
        factor[:rank, part] = high
        factor[rank:, part] = low
        tensor_copy(k).wait()
        high, low = split(tensor[part])
        first = jnp.dot(factor[:, part], high, preferred_element_type=jnp.float32)
        second = jnp.dot(factor[:rank, part], low, preferred_element_type=jnp.float32)
        term = first[:rank] + first[rank:] + second
        if k == 0:
            total[...] = term
        else:
            total[...] += term
    for d in range(nodes):
        outs[d][...] = total[pl.ds(pl.multiple_of((node[0] ^ d) * rows, rows), rows)]


def project(tensor, basis, node, nodes):
    _, depth, width = tensor.shape
    rank = basis.shape[1]
    chunk = depth // 8
    return pl.pallas_call(
        functools.partial(project_kernel, chunk, nodes),
        in_specs=[pl.BlockSpec(memory_space=pltpu.SMEM)] + [pl.BlockSpec(memory_space=pl.ANY)] * 2,
        out_specs=[pl.BlockSpec(memory_space=pltpu.VMEM)] * nodes,
        out_shape=[jax.ShapeDtypeStruct((rank // nodes, width), jnp.float32)] * nodes,
        scratch_shapes=[
            pltpu.VMEM((depth, rank), jnp.float32),
            pltpu.VMEM((depth, width), jnp.float32),
            pltpu.VMEM((2 * rank, depth), jnp.bfloat16),
            pltpu.VMEM((rank, width), jnp.float32),
            pltpu.SemaphoreType.DMA((8,)),
            pltpu.SemaphoreType.DMA((8,)),
        ],
        compiler_params=pltpu.CompilerParams(vmem_limit_bytes=VMEM_LIMIT),
        cost_estimate=pl.CostEstimate(
            flops=6 * rank * depth * width, bytes_accessed=4 * depth * (width + rank), transcendentals=0
        ),
        name="project",
    )(node, basis, tensor)


def gram_kernel(nodes, groups, cols, scale, place, *refs):
    half = nodes // 2
    share, refs = refs[0], refs[1:]
    near, near_swap, refs = refs[: half - 1], refs[half - 1 : nodes - 2], refs[nodes - 2 :]
    far, far_swap, refs = refs[0], refs[1], refs[2:]
    come, come_swap, refs = refs[:half], refs[half:nodes], refs[nodes:]
    out, left, right_high, right_low = refs
    rows, width = share.shape
    step = pl.program_id(0)
    core = place[0]

    def slot(index):
        return pl.ds(pl.multiple_of(index * rows, rows), rows)

    def columns(index, size):
        return pl.ds(pl.multiple_of(index * size, size), size)

    @pl.when(step == 0)
    def _():
        left[:rows] = share[...]
        for k in range(half - 1):
            left[slot(2 * k + 1 + core)] = near[k][...]
            left[slot(2 * k + 2 - core)] = near_swap[k][...]
        left[(nodes - 1) * rows :, columns(core, width // 2)] = far[...]
        left[(nodes - 1) * rows :, columns(1 - core, width // 2)] = far_swap[...]

    @pl.when((step == 0) & (place[2] == 1))
    def _():
        high, low = split(left[:, columns(place[1] * 2 + core, cols)])
        right_high[...] = high
        right_low[...] = low

    @pl.when((step == 0) & (place[2] != 1))
    def _():
        for k in range(half):
            high, low = split(come[k][:, columns(core, cols)])
            right_high[slot(place[3 + k])] = high
            right_low[slot(place[3 + k])] = low
            high, low = split(come_swap[k][...])
            right_high[slot(place[3 + half + k])] = high
            right_low[slot(place[3 + half + k])] = low

    size = out.shape[0]
    high, low = split(left[:, columns(step, size)].T)
    term = jnp.dot(high, right_high[...], preferred_element_type=jnp.float32)
    term += jnp.dot(low, right_high[...], preferred_element_type=jnp.float32)
    term += jnp.dot(high, right_low[...], preferred_element_type=jnp.float32)
    out[...] = term * scale


def gram_block(place, share, near, near_swap, far, far_swap, come, come_swap, nodes, groups, cols, scale):
    rows, width = share.shape
    depth = nodes * rows
    size = width // 2
    arrays = (share, *near, *near_swap, far, far_swap, *come, *come_swap)
    return pl.pallas_call(
        functools.partial(gram_kernel, nodes, groups, cols, scale),
        grid_spec=pltpu.PrefetchScalarGridSpec(
            num_scalar_prefetch=1,
            grid=(width // size,),
            in_specs=[pl.BlockSpec(x.shape, lambda s, place: (0, 0)) for x in arrays],
            out_specs=pl.BlockSpec((size, cols), lambda s, place: (s, 0)),
            scratch_shapes=[
                pltpu.VMEM((depth, width), jnp.float32),
                pltpu.VMEM((depth, cols), jnp.bfloat16),
                pltpu.VMEM((depth, cols), jnp.bfloat16),
            ],
        ),
        out_shape=jax.ShapeDtypeStruct((width, cols), jnp.float32),
        compiler_params=pltpu.CompilerParams(vmem_limit_bytes=24 * 1024 * 1024),
        cost_estimate=pl.CostEstimate(
            flops=6 * depth * width * cols, bytes_accessed=4 * width * cols, transcendentals=0
        ),
        name="gram",
    )(place, *arrays)


def gray(n):
    return n ^ (n >> 1)


def body(tensor, basis):
    nodes, feats, cores = lax.axis_size("node"), lax.axis_size("feat"), lax.axis_size("tm")
    rank = basis.shape[1]
    width = tensor.shape[2]
    groups = nodes // feats
    rows = rank // nodes
    cols = width // (groups * cores)
    scale = 1.0 / (rank * cores)
    half = nodes // 2
    node, feat, core = lax.axis_index("node"), lax.axis_index("feat"), lax.axis_index("tm")
    everyone = ("node", "feat", "tm")

    def device(n, z, c):
        return (n * feats + z) * cores + c

    def swap(x):
        return lax.ppermute(x, "tm", [(0, 1), (1, 0)])

    pieces = project(tensor, basis, node.astype(jnp.int32).reshape(1), nodes)
    share = pieces[0]
    for d in range(1, nodes):
        share += lax.ppermute(pieces[d], "node", [(n, n ^ d) for n in range(nodes)])
    share = lax.all_gather(share, "tm", axis=0, tiled=True)

    targets = (feats - 1) * groups
    table = [0] * nodes
    for idx in range(targets):
        table[gray(idx)] = idx % groups
    come = []
    for k in range(half):
        pairs = []
        for c in range(cores):
            for z in range(feats):
                for idx in range(targets):
                    source = (z * groups) ^ (k + c * half) ^ gray(idx)
                    d, g = idx // groups + 1, idx % groups
                    pairs.append((device(source, z, c), device(z * groups + g, z ^ d, c)))
        if groups == 1:
            part = share
        else:
            g = jnp.asarray(table)[node ^ (feat * groups) ^ (k + core * half)]
            part = lax.dynamic_slice_in_dim(share, g * cores * cols, cores * cols, 1)
        come.append(lax.ppermute(part, everyone, pairs))

    near = []
    for k in range(half - 1):
        pairs = [
            (device(n, z, c), device(n ^ (2 * k + 1 + c), z, c))
            for c in range(cores)
            for n in range(nodes)
            for z in range(feats)
        ]
        near.append(lax.ppermute(share, everyone, pairs))
    part = lax.dynamic_slice_in_dim(share, core * (width // 2), width // 2, 1)
    far = lax.ppermute(part, "node", [(n, n ^ (nodes - 1)) for n in range(nodes)])

    near_swap = [swap(x) for x in near]
    far_swap = swap(far)
    come_swap = [swap(lax.dynamic_slice_in_dim(x, (1 - core) * cols, cols, 1)) for x in come]

    block, g = node // groups, node % groups
    idx = ((feat ^ block) - 1) * groups + g
    base = gray(idx) ^ (block * groups) ^ node
    slots = [(k + core * half) ^ base for k in range(half)] + [(k + (1 - core) * half) ^ base for k in range(half)]
    place = jnp.stack([core, g, (block == feat).astype(jnp.int32), *slots]).astype(jnp.int32)
    return gram_block(place, share, near, near_swap, far, far_swap, come, come_swap, nodes, groups, cols, scale)


def solution(mesh):
    in_specs = (P("tm", "node", "feat"), P("node", None))
    out_specs = P("feat", ("node", "tm"))
    return jax.shard_map(body, mesh=mesh, in_specs=in_specs, out_specs=out_specs, check_vma=False)
```

```python
import functools

import jax
import jax.numpy as jnp
from jax import lax
from jax.experimental import pallas as pl
from jax.experimental.pallas import tpu as pltpu
from jax.sharding import PartitionSpec as P

VMEM_LIMIT = 52 * 1024 * 1024


def split(x):
    high = x.astype(jnp.bfloat16)
    return high, (x - high.astype(jnp.float32)).astype(jnp.bfloat16)


def project_kernel(chunk, nodes, node, basis_hbm, tensor_hbm, *refs):
    outs = refs[:nodes]
    basis, tensor, factor, total, basis_sem, tensor_sem = refs[nodes:]
    depth, width = tensor.shape
    rank = basis.shape[1]
    rows = rank // nodes
    count = depth // chunk

    def basis_copy(k):
        part = pl.ds(k * chunk, chunk)
        return pltpu.make_async_copy(basis_hbm.at[part], basis.at[part], basis_sem.at[k])

    def tensor_copy(k):
        part = pl.ds(k * chunk, chunk)
        return pltpu.make_async_copy(tensor_hbm.at[0, part], tensor.at[part], tensor_sem.at[k])

    for k in range(count):
        basis_copy(k).start()
        tensor_copy(k).start()
    for k in range(count):
        part = slice(k * chunk, (k + 1) * chunk)
        basis_copy(k).wait()
        high, low = split(basis[part].T)
        factor[:rank, part] = high
        factor[rank:, part] = low
        tensor_copy(k).wait()
        high, low = split(tensor[part])
        first = jnp.dot(factor[:, part], high, preferred_element_type=jnp.float32)
        second = jnp.dot(factor[:rank, part], low, preferred_element_type=jnp.float32)
        term = first[:rank] + first[rank:] + second
        if k == 0:
            total[...] = term
        else:
            total[...] += term
    for d in range(nodes):
        outs[d][...] = total[pl.ds(pl.multiple_of((node[0] ^ d) * rows, rows), rows)]


def project(tensor, basis, node, nodes):
    _, depth, width = tensor.shape
    rank = basis.shape[1]
    chunk = depth // 8
    return pl.pallas_call(
        functools.partial(project_kernel, chunk, nodes),
        in_specs=[pl.BlockSpec(memory_space=pltpu.SMEM)] + [pl.BlockSpec(memory_space=pl.ANY)] * 2,
        out_specs=[pl.BlockSpec(memory_space=pltpu.VMEM)] * nodes,
        out_shape=[jax.ShapeDtypeStruct((rank // nodes, width), jnp.float32)] * nodes,
        scratch_shapes=[
            pltpu.VMEM((depth, rank), jnp.float32),
            pltpu.VMEM((depth, width), jnp.float32),
            pltpu.VMEM((2 * rank, depth), jnp.bfloat16),
            pltpu.VMEM((rank, width), jnp.float32),
            pltpu.SemaphoreType.DMA((8,)),
            pltpu.SemaphoreType.DMA((8,)),
        ],
        compiler_params=pltpu.CompilerParams(vmem_limit_bytes=VMEM_LIMIT),
        cost_estimate=pl.CostEstimate(
            flops=6 * rank * depth * width, bytes_accessed=4 * depth * (width + rank), transcendentals=0
        ),
        name="project",
    )(node, basis, tensor)


def gram_kernel(nodes, groups, cols, scale, place, *refs):
    half = nodes // 2
    share, refs = refs[0], refs[1:]
    near, near_swap, refs = refs[: half - 1], refs[half - 1 : nodes - 2], refs[nodes - 2 :]
    far, far_swap, refs = refs[0], refs[1], refs[2:]
    come, come_swap, refs = refs[:half], refs[half:nodes], refs[nodes:]
    out_hbm, out, left, right_high, right_low, sem = refs
    rows, width = share.shape
    size = min(width, 256)
    core = place[0]

    def slot(index):
        return pl.ds(pl.multiple_of(index * rows, rows), rows)

    def columns(index, size):
        return pl.ds(pl.multiple_of(index * size, size), size)

    left[:rows] = share[...]
    for k in range(half - 1):
        left[slot(2 * k + 1 + core)] = near[k][...]
        left[slot(2 * k + 2 - core)] = near_swap[k][...]
    left[(nodes - 1) * rows :, columns(core, width // 2)] = far[...]
    left[(nodes - 1) * rows :, columns(1 - core, width // 2)] = far_swap[...]

    @pl.when(place[2] == 1)
    def _():
        high, low = split(left[:, columns(place[1] * 2 + core, cols)])
        right_high[...] = high
        right_low[...] = low

    @pl.when(place[2] != 1)
    def _():
        for k in range(half):
            high, low = split(come[k][:, columns(core, cols)])
            right_high[slot(place[3 + k])] = high
            right_low[slot(place[3 + k])] = low
            high, low = split(come_swap[k][...])
            right_high[slot(place[3 + half + k])] = high
            right_low[slot(place[3 + half + k])] = low

    copies = []
    for k in range(width // size):
        part = pl.ds(k * size, size)
        high, low = split(left[:, k * size : (k + 1) * size].T)
        term = jnp.dot(high, right_high[...], preferred_element_type=jnp.float32)
        term += jnp.dot(low, right_high[...], preferred_element_type=jnp.float32)
        term += jnp.dot(high, right_low[...], preferred_element_type=jnp.float32)
        out[part] = term * scale
        copies.append(pltpu.make_async_copy(out.at[part], out_hbm.at[part], sem.at[k]))
        copies[-1].start()
    for copy in copies:
        copy.wait()


def gram_block(place, share, near, near_swap, far, far_swap, come, come_swap, nodes, groups, cols, scale):
    rows, width = share.shape
    depth = nodes * rows
    arrays = (share, *near, *near_swap, far, far_swap, *come, *come_swap)
    return pl.pallas_call(
        functools.partial(gram_kernel, nodes, groups, cols, scale),
        in_specs=[pl.BlockSpec(memory_space=pltpu.SMEM)] + [pl.BlockSpec(memory_space=pltpu.VMEM)] * len(arrays),
        out_specs=pl.BlockSpec(memory_space=pl.ANY),
        out_shape=jax.ShapeDtypeStruct((width, cols), jnp.float32),
        scratch_shapes=[
            pltpu.VMEM((width, cols), jnp.float32),
            pltpu.VMEM((depth, width), jnp.float32),
            pltpu.VMEM((depth, cols), jnp.bfloat16),
            pltpu.VMEM((depth, cols), jnp.bfloat16),
            pltpu.SemaphoreType.DMA((width // min(width, 256),)),
        ],
        compiler_params=pltpu.CompilerParams(vmem_limit_bytes=24 * 1024 * 1024),
        cost_estimate=pl.CostEstimate(
            flops=6 * depth * width * cols, bytes_accessed=4 * width * cols, transcendentals=0
        ),
        name="gram",
    )(place, *arrays)


def gray(n):
    return n ^ (n >> 1)


def body(tensor, basis):
    nodes, feats, cores = lax.axis_size("node"), lax.axis_size("feat"), lax.axis_size("tm")
    rank = basis.shape[1]
    width = tensor.shape[2]
    groups = nodes // feats
    rows = rank // nodes
    cols = width // (groups * cores)
    scale = 1.0 / (rank * cores)
    half = nodes // 2
    node, feat, core = lax.axis_index("node"), lax.axis_index("feat"), lax.axis_index("tm")
    everyone = ("node", "feat", "tm")

    def device(n, z, c):
        return (n * feats + z) * cores + c

    def swap(x):
        return lax.ppermute(x, "tm", [(0, 1), (1, 0)])

    pieces = project(tensor, basis, node.astype(jnp.int32).reshape(1), nodes)
    share = pieces[0]
    for d in range(1, nodes):
        share += lax.ppermute(pieces[d], "node", [(n, n ^ d) for n in range(nodes)])
    both = lax.ppermute(share, "tm", [(0, 1), (1, 0)])
    share = jnp.where(core == 0, jnp.concatenate([share, both]), jnp.concatenate([both, share]))

    targets = (feats - 1) * groups
    table = [0] * nodes
    for idx in range(targets):
        table[gray(idx)] = idx % groups
    come = []
    for k in range(half):
        pairs = []
        for c in range(cores):
            for z in range(feats):
                for idx in range(targets):
                    source = (z * groups) ^ (k + c * half) ^ gray(idx)
                    d, g = idx // groups + 1, idx % groups
                    pairs.append((device(source, z, c), device(z * groups + g, z ^ d, c)))
        if groups == 1:
            part = share
        else:
            g = jnp.asarray(table)[node ^ (feat * groups) ^ (k + core * half)]
            part = lax.dynamic_slice_in_dim(share, g * cores * cols, cores * cols, 1)
        come.append(lax.ppermute(part, everyone, pairs))

    near = []
    for k in range(half - 1):
        pairs = [
            (device(n, z, c), device(n ^ (2 * k + 1 + c), z, c))
            for c in range(cores)
            for n in range(nodes)
            for z in range(feats)
        ]
        near.append(lax.ppermute(share, everyone, pairs))
    part = lax.dynamic_slice_in_dim(share, core * (width // 2), width // 2, 1)
    far = lax.ppermute(part, "node", [(n, n ^ (nodes - 1)) for n in range(nodes)])

    near_swap = [swap(x) for x in near]
    far_swap = swap(far)
    come_swap = [swap(lax.dynamic_slice_in_dim(x, (1 - core) * cols, cols, 1)) for x in come]

    block, g = node // groups, node % groups
    idx = ((feat ^ block) - 1) * groups + g
    base = gray(idx) ^ (block * groups) ^ node
    slots = [(k + core * half) ^ base for k in range(half)] + [(k + (1 - core) * half) ^ base for k in range(half)]
    place = jnp.stack([core, g, (block == feat).astype(jnp.int32), *slots]).astype(jnp.int32)
    return gram_block(place, share, near, near_swap, far, far_swap, come, come_swap, nodes, groups, cols, scale)


def solution(mesh):
    in_specs = (P("tm", "node", "feat"), P("node", None))
    out_specs = P("feat", ("node", "tm"))
    return jax.shard_map(body, mesh=mesh, in_specs=in_specs, out_specs=out_specs, check_vma=False)
```

```python
import functools

import jax
import jax.numpy as jnp
from jax import lax
from jax.experimental import pallas as pl
from jax.experimental.pallas import tpu as pltpu
from jax.sharding import PartitionSpec as P

VMEM_LIMIT = 52 * 1024 * 1024


def split(x):
    high = x.astype(jnp.bfloat16)
    return high, (x - high.astype(jnp.float32)).astype(jnp.bfloat16)


def project_kernel(chunk, nodes, node, basis_hbm, tensor_hbm, *refs):
    outs = refs[:nodes]
    basis, tensor, factor, total, basis_sem, tensor_sem = refs[nodes:]
    depth, width = tensor.shape
    rank = basis.shape[1]
    rows = rank // nodes
    count = depth // chunk

    def basis_copy(k):
        part = pl.ds(k * chunk, chunk)
        return pltpu.make_async_copy(basis_hbm.at[part], basis.at[part], basis_sem.at[k])

    def tensor_copy(k):
        part = pl.ds(k * chunk, chunk)
        return pltpu.make_async_copy(tensor_hbm.at[0, part], tensor.at[part], tensor_sem.at[k])

    for k in range(count):
        basis_copy(k).start()
        tensor_copy(k).start()
    for k in range(count):
        part = slice(k * chunk, (k + 1) * chunk)
        basis_copy(k).wait()
        high, low = split(basis[part].T)
        factor[:rank, part] = high
        factor[rank:, part] = low
        tensor_copy(k).wait()
        high, low = split(tensor[part])
        first = jnp.dot(factor[:, part], high, preferred_element_type=jnp.float32)
        second = jnp.dot(factor[:rank, part], low, preferred_element_type=jnp.float32)
        term = first[:rank] + first[rank:] + second
        if k == 0:
            total[...] = term
        else:
            total[...] += term
    for d in range(nodes):
        outs[d][...] = total[pl.ds(pl.multiple_of((node[0] ^ d) * rows, rows), rows)]


def project(tensor, basis, node, nodes):
    _, depth, width = tensor.shape
    rank = basis.shape[1]
    chunk = depth // 8
    return pl.pallas_call(
        functools.partial(project_kernel, chunk, nodes),
        in_specs=[pl.BlockSpec(memory_space=pltpu.SMEM)] + [pl.BlockSpec(memory_space=pl.ANY)] * 2,
        out_specs=[pl.BlockSpec(memory_space=pltpu.VMEM)] * nodes,
        out_shape=[jax.ShapeDtypeStruct((rank // nodes, width), jnp.float32)] * nodes,
        scratch_shapes=[
            pltpu.VMEM((depth, rank), jnp.float32),
            pltpu.VMEM((depth, width), jnp.float32),
            pltpu.VMEM((2 * rank, depth), jnp.bfloat16),
            pltpu.VMEM((rank, width), jnp.float32),
            pltpu.SemaphoreType.DMA((8,)),
            pltpu.SemaphoreType.DMA((8,)),
        ],
        compiler_params=pltpu.CompilerParams(vmem_limit_bytes=VMEM_LIMIT),
        cost_estimate=pl.CostEstimate(
            flops=6 * rank * depth * width, bytes_accessed=4 * depth * (width + rank), transcendentals=0
        ),
        name="project",
    )(node, basis, tensor)


def gram_kernel(nodes, groups, cols, scale, place, *refs):
    half = nodes // 2
    share, refs = refs[0], refs[1:]
    near, near_swap, refs = refs[: half - 1], refs[half - 1 : nodes - 2], refs[nodes - 2 :]
    far, far_swap, refs = refs[0], refs[1], refs[2:]
    come, come_swap, refs = refs[:half], refs[half:nodes], refs[nodes:]
    out_hbm, out, left, right_high, right_low, sem = refs
    rows, width = share.shape
    size = min(width, 256)
    core = place[0]

    def slot(index):
        return pl.ds(pl.multiple_of(index * rows, rows), rows)

    def columns(index, size):
        return pl.ds(pl.multiple_of(index * size, size), size)

    left[:rows] = share[...]
    for k in range(half - 1):
        left[slot(2 * k + 1 + core)] = near[k][...]
        left[slot(2 * k + 2 - core)] = near_swap[k][...]
    left[(nodes - 1) * rows :, columns(core, width // 2)] = far[...]
    left[(nodes - 1) * rows :, columns(1 - core, width // 2)] = far_swap[...]

    @pl.when(place[2] == 1)
    def _():
        high, low = split(left[:, columns(place[1] * 2 + core, cols)])
        right_high[...] = high
        right_low[...] = low

    @pl.when(place[2] != 1)
    def _():
        for k in range(half):
            high, low = split(come[k][:, columns(core, cols)])
            right_high[slot(place[3 + k])] = high
            right_low[slot(place[3 + k])] = low
            high, low = split(come_swap[k][...])
            right_high[slot(place[3 + half + k])] = high
            right_low[slot(place[3 + half + k])] = low

    copies = []
    for k in range(width // size):
        part = pl.ds(k * size, size)
        high, low = split(left[:, k * size : (k + 1) * size])
        dims = (((0,), (0,)), ((), ()))
        term = lax.dot_general(high, right_high[...], dims, preferred_element_type=jnp.float32)
        term += lax.dot_general(low, right_high[...], dims, preferred_element_type=jnp.float32)
        term += lax.dot_general(high, right_low[...], dims, preferred_element_type=jnp.float32)
        out[part] = term * scale
        copies.append(pltpu.make_async_copy(out.at[part], out_hbm.at[part], sem.at[k]))
        copies[-1].start()
    for copy in copies:
        copy.wait()


def gram_block(place, share, near, near_swap, far, far_swap, come, come_swap, nodes, groups, cols, scale):
    rows, width = share.shape
    depth = nodes * rows
    arrays = (share, *near, *near_swap, far, far_swap, *come, *come_swap)
    return pl.pallas_call(
        functools.partial(gram_kernel, nodes, groups, cols, scale),
        in_specs=[pl.BlockSpec(memory_space=pltpu.SMEM)] + [pl.BlockSpec(memory_space=pltpu.VMEM)] * len(arrays),
        out_specs=pl.BlockSpec(memory_space=pl.ANY),
        out_shape=jax.ShapeDtypeStruct((width, cols), jnp.float32),
        scratch_shapes=[
            pltpu.VMEM((width, cols), jnp.float32),
            pltpu.VMEM((depth, width), jnp.float32),
            pltpu.VMEM((depth, cols), jnp.bfloat16),
            pltpu.VMEM((depth, cols), jnp.bfloat16),
            pltpu.SemaphoreType.DMA((width // min(width, 256),)),
        ],
        compiler_params=pltpu.CompilerParams(vmem_limit_bytes=24 * 1024 * 1024),
        cost_estimate=pl.CostEstimate(
            flops=6 * depth * width * cols, bytes_accessed=4 * width * cols, transcendentals=0
        ),
        name="gram",
    )(place, *arrays)


def gray(n):
    return n ^ (n >> 1)


def body(tensor, basis):
    nodes, feats, cores = lax.axis_size("node"), lax.axis_size("feat"), lax.axis_size("tm")
    rank = basis.shape[1]
    width = tensor.shape[2]
    groups = nodes // feats
    rows = rank // nodes
    cols = width // (groups * cores)
    scale = 1.0 / (rank * cores)
    half = nodes // 2
    node, feat, core = lax.axis_index("node"), lax.axis_index("feat"), lax.axis_index("tm")
    everyone = ("node", "feat", "tm")

    def device(n, z, c):
        return (n * feats + z) * cores + c

    def swap(x):
        return lax.ppermute(x, "tm", [(0, 1), (1, 0)])

    pieces = project(tensor, basis, node.astype(jnp.int32).reshape(1), nodes)
    share = pieces[0]
    for d in range(1, nodes):
        share += lax.ppermute(pieces[d], "node", [(n, n ^ d) for n in range(nodes)])
    both = lax.ppermute(share, "tm", [(0, 1), (1, 0)])
    share = jnp.where(core == 0, jnp.concatenate([share, both]), jnp.concatenate([both, share]))

    targets = (feats - 1) * groups
    table = [0] * nodes
    for idx in range(targets):
        table[gray(idx)] = idx % groups
    come = []
    for k in range(half):
        pairs = []
        for c in range(cores):
            for z in range(feats):
                for idx in range(targets):
                    source = (z * groups) ^ (k ^ (c * (nodes - 1))) ^ gray(idx)
                    d, g = idx // groups + 1, idx % groups
                    pairs.append((device(source, z, c), device(z * groups + g, z ^ d, c)))
        if groups == 1:
            part = share
        else:
            g = jnp.asarray(table)[node ^ (feat * groups) ^ (k ^ (core * (nodes - 1)))]
            part = lax.dynamic_slice_in_dim(share, g * cores * cols, cores * cols, 1)
        come.append(lax.ppermute(part, everyone, pairs))

    near = []
    for k in range(half - 1):
        pairs = [
            (device(n, z, c), device(n ^ (2 * k + 1 + c), z, c))
            for c in range(cores)
            for n in range(nodes)
            for z in range(feats)
        ]
        near.append(lax.ppermute(share, everyone, pairs))
    part = lax.dynamic_slice_in_dim(share, core * (width // 2), width // 2, 1)
    far = lax.ppermute(part, "node", [(n, n ^ (nodes - 1)) for n in range(nodes)])

    near_swap = [swap(x) for x in near]
    far_swap = swap(far)
    come_swap = [swap(lax.dynamic_slice_in_dim(x, (1 - core) * cols, cols, 1)) for x in come]

    block, g = node // groups, node % groups
    idx = ((feat ^ block) - 1) * groups + g
    base = gray(idx) ^ (block * groups) ^ node
    slots = [(k ^ (core * (nodes - 1))) ^ base for k in range(half)] + [(k ^ ((1 - core) * (nodes - 1))) ^ base for k in range(half)]
    place = jnp.stack([core, g, (block == feat).astype(jnp.int32), *slots]).astype(jnp.int32)
    return gram_block(place, share, near, near_swap, far, far_swap, come, come_swap, nodes, groups, cols, scale)


def solution(mesh):
    in_specs = (P("tm", "node", "feat"), P("node", None))
    out_specs = P("feat", ("node", "tm"))
    return jax.shard_map(body, mesh=mesh, in_specs=in_specs, out_specs=out_specs, check_vma=False)
```

```python
import functools

import jax
import jax.numpy as jnp
from jax import lax
from jax.experimental import pallas as pl
from jax.experimental.pallas import tpu as pltpu
from jax.sharding import PartitionSpec as P

VMEM_LIMIT = 52 * 1024 * 1024


def split(x):
    high = x.astype(jnp.bfloat16)
    return high, (x - high.astype(jnp.float32)).astype(jnp.bfloat16)


def project_kernel(chunk, nodes, node, basis_hbm, tensor_hbm, *refs):
    outs = refs[:nodes]
    basis, tensor, factor, total, basis_sem, tensor_sem = refs[nodes:]
    depth, width = tensor.shape
    rank = basis.shape[1]
    rows = rank // nodes
    count = depth // chunk

    def basis_copy(k):
        part = pl.ds(k * chunk, chunk)
        return pltpu.make_async_copy(basis_hbm.at[part], basis.at[part], basis_sem.at[k])

    def tensor_copy(k):
        part = pl.ds(k * chunk, chunk)
        return pltpu.make_async_copy(tensor_hbm.at[0, part], tensor.at[part], tensor_sem.at[k])

    for k in range(count):
        basis_copy(k).start()
        tensor_copy(k).start()
    for k in range(count):
        part = slice(k * chunk, (k + 1) * chunk)
        basis_copy(k).wait()
        high, low = split(basis[part].T)
        factor[:rank, part] = high
        factor[rank:, part] = low
        tensor_copy(k).wait()
        high, low = split(tensor[part])
        first = jnp.dot(factor[:, part], high, preferred_element_type=jnp.float32)
        second = jnp.dot(factor[:rank, part], low, preferred_element_type=jnp.float32)
        term = first[:rank] + first[rank:] + second
        if k == 0:
            total[...] = term
        else:
            total[...] += term
    for d in range(nodes):
        outs[d][...] = total[pl.ds(pl.multiple_of((node[0] ^ d) * rows, rows), rows)]


def project(tensor, basis, node, nodes):
    _, depth, width = tensor.shape
    rank = basis.shape[1]
    chunk = depth // 8
    return pl.pallas_call(
        functools.partial(project_kernel, chunk, nodes),
        in_specs=[pl.BlockSpec(memory_space=pltpu.SMEM)] + [pl.BlockSpec(memory_space=pl.ANY)] * 2,
        out_specs=[pl.BlockSpec(memory_space=pltpu.VMEM)] * nodes,
        out_shape=[jax.ShapeDtypeStruct((rank // nodes, width), jnp.float32)] * nodes,
        scratch_shapes=[
            pltpu.VMEM((depth, rank), jnp.float32),
            pltpu.VMEM((depth, width), jnp.float32),
            pltpu.VMEM((2 * rank, depth), jnp.bfloat16),
            pltpu.VMEM((rank, width), jnp.float32),
            pltpu.SemaphoreType.DMA((8,)),
            pltpu.SemaphoreType.DMA((8,)),
        ],
        compiler_params=pltpu.CompilerParams(vmem_limit_bytes=VMEM_LIMIT),
        cost_estimate=pl.CostEstimate(
            flops=6 * rank * depth * width, bytes_accessed=4 * depth * (width + rank), transcendentals=0
        ),
        name="project",
    )(node, basis, tensor)


def gram_kernel(nodes, groups, cols, scale, place, *refs):
    half = nodes // 2
    share, refs = refs[0], refs[1:]
    near, near_swap, refs = refs[: half - 1], refs[half - 1 : nodes - 2], refs[nodes - 2 :]
    far, far_swap, refs = refs[0], refs[1], refs[2:]
    come, come_swap, refs = refs[:half], refs[half:nodes], refs[nodes:]
    out_hbm, out, left, right_high, right_low, sem = refs
    rows, width = share.shape
    size = min(width, 128)
    core = place[0]

    def slot(index):
        return pl.ds(pl.multiple_of(index * rows, rows), rows)

    def columns(index, size):
        return pl.ds(pl.multiple_of(index * size, size), size)

    left[:rows] = share[...]
    for k in range(half - 1):
        left[slot(2 * k + 1 + core)] = near[k][...]
        left[slot(2 * k + 2 - core)] = near_swap[k][...]
    left[(nodes - 1) * rows :, columns(core, width // 2)] = far[...]
    left[(nodes - 1) * rows :, columns(1 - core, width // 2)] = far_swap[...]

    @pl.when(place[2] == 1)
    def _():
        high, low = split(left[:, columns(place[1] * 2 + core, cols)] * scale)
        right_high[...] = high
        right_low[...] = low

    @pl.when(place[2] != 1)
    def _():
        for k in range(half):
            high, low = split(come[k][:, columns(core, cols)] * scale)
            right_high[slot(place[3 + k])] = high
            right_low[slot(place[3 + k])] = low
            high, low = split(come_swap[k][...] * scale)
            right_high[slot(place[3 + half + k])] = high
            right_low[slot(place[3 + half + k])] = low

    copies = []
    for k in range(width // size):
        part = pl.ds(k * size, size)
        high, low = split(left[:, k * size : (k + 1) * size])
        dims = (((0,), (0,)), ((), ()))
        term = lax.dot_general(high, right_high[...], dims, preferred_element_type=jnp.float32)
        term += lax.dot_general(low, right_high[...], dims, preferred_element_type=jnp.float32)
        term += lax.dot_general(high, right_low[...], dims, preferred_element_type=jnp.float32)
        out[part] = term
        copies.append(pltpu.make_async_copy(out.at[part], out_hbm.at[part], sem.at[k]))
        copies[-1].start()
    for copy in copies:
        copy.wait()


def gram_block(place, share, near, near_swap, far, far_swap, come, come_swap, nodes, groups, cols, scale):
    rows, width = share.shape
    depth = nodes * rows
    arrays = (share, *near, *near_swap, far, far_swap, *come, *come_swap)
    return pl.pallas_call(
        functools.partial(gram_kernel, nodes, groups, cols, scale),
        in_specs=[pl.BlockSpec(memory_space=pltpu.SMEM)] + [pl.BlockSpec(memory_space=pltpu.VMEM)] * len(arrays),
        out_specs=pl.BlockSpec(memory_space=pl.ANY),
        out_shape=jax.ShapeDtypeStruct((width, cols), jnp.float32),
        scratch_shapes=[
            pltpu.VMEM((width, cols), jnp.float32),
            pltpu.VMEM((depth, width), jnp.float32),
            pltpu.VMEM((depth, cols), jnp.bfloat16),
            pltpu.VMEM((depth, cols), jnp.bfloat16),
            pltpu.SemaphoreType.DMA((width // min(width, 128),)),
        ],
        compiler_params=pltpu.CompilerParams(vmem_limit_bytes=24 * 1024 * 1024),
        cost_estimate=pl.CostEstimate(
            flops=6 * depth * width * cols, bytes_accessed=4 * width * cols, transcendentals=0
        ),
        name="gram",
    )(place, *arrays)


def gray(n):
    return n ^ (n >> 1)


def body(tensor, basis):
    nodes, feats, cores = lax.axis_size("node"), lax.axis_size("feat"), lax.axis_size("tm")
    rank = basis.shape[1]
    width = tensor.shape[2]
    groups = nodes // feats
    rows = rank // nodes
    cols = width // (groups * cores)
    scale = 1.0 / (rank * cores)
    half = nodes // 2
    node, feat, core = lax.axis_index("node"), lax.axis_index("feat"), lax.axis_index("tm")
    everyone = ("node", "feat", "tm")

    def device(n, z, c):
        return (n * feats + z) * cores + c

    def swap(x):
        return lax.ppermute(x, "tm", [(0, 1), (1, 0)])

    pieces = project(tensor, basis, node.astype(jnp.int32).reshape(1), nodes)
    share = pieces[0]
    for d in range(1, nodes):
        share += lax.ppermute(pieces[d], "node", [(n, n ^ d) for n in range(nodes)])
    both = lax.ppermute(share, "tm", [(0, 1), (1, 0)])
    share = jnp.where(core == 0, jnp.concatenate([share, both]), jnp.concatenate([both, share]))

    targets = (feats - 1) * groups
    table = [0] * nodes
    for idx in range(targets):
        table[gray(idx)] = idx % groups
    come = []
    for k in range(half):
        pairs = []
        for c in range(cores):
            for z in range(feats):
                for idx in range(targets):
                    source = (z * groups) ^ (k ^ (c * (nodes - 1))) ^ gray(idx)
                    d, g = idx // groups + 1, idx % groups
                    pairs.append((device(source, z, c), device(z * groups + g, z ^ d, c)))
        if groups == 1:
            part = share
        else:
            g = jnp.asarray(table)[node ^ (feat * groups) ^ (k ^ (core * (nodes - 1)))]
            part = lax.dynamic_slice_in_dim(share, g * cores * cols, cores * cols, 1)
        come.append(lax.ppermute(part, everyone, pairs))

    near = []
    for k in range(half - 1):
        pairs = [
            (device(n, z, c), device(n ^ (2 * k + 1 + c), z, c))
            for c in range(cores)
            for n in range(nodes)
            for z in range(feats)
        ]
        near.append(lax.ppermute(share, everyone, pairs))
    part = lax.dynamic_slice_in_dim(share, core * (width // 2), width // 2, 1)
    far = lax.ppermute(part, "node", [(n, n ^ (nodes - 1)) for n in range(nodes)])

    near_swap = [swap(x) for x in near]
    far_swap = swap(far)
    come_swap = [swap(lax.dynamic_slice_in_dim(x, (1 - core) * cols, cols, 1)) for x in come]

    block, g = node // groups, node % groups
    idx = ((feat ^ block) - 1) * groups + g
    base = gray(idx) ^ (block * groups) ^ node
    slots = [(k ^ (core * (nodes - 1))) ^ base for k in range(half)] + [(k ^ ((1 - core) * (nodes - 1))) ^ base for k in range(half)]
    place = jnp.stack([core, g, (block == feat).astype(jnp.int32), *slots]).astype(jnp.int32)
    return gram_block(place, share, near, near_swap, far, far_swap, come, come_swap, nodes, groups, cols, scale)


def solution(mesh):
    in_specs = (P("tm", "node", "feat"), P("node", None))
    out_specs = P("feat", ("node", "tm"))
    return jax.shard_map(body, mesh=mesh, in_specs=in_specs, out_specs=out_specs, check_vma=False)
```
